32 devices in a mesh: ctx: 8 (over z, y), dp: 4 (over x, core).
Axes of the slice: x: 2, y: 2, z: 4, core: 2. Of those that a mesh axis runs over, the one named last changes fastest.
Arguments:
- tokens: bfloat16 [8, 512, 4096], P('dp', 'ctx'), may hold values from -6 to 6
- queries: bfloat16 [8, 512, 2048], P('dp', 'ctx'), may hold values from -160 to 160
- d_attended: bfloat16 [8, 512, 2048], P('dp', 'ctx'), may hold values from -6 to 6
- span_order: int32 [16], replicated, may hold values from 0 to 15, each once
- norm_gain: float32 [4096], replicated, may hold values from 0.1 to 1.9
- key_weight: bfloat16 [4096, 512], replicated, may hold values from -0.09375 to 0.09375
- value_weight: bfloat16 [4096, 512], replicated, may hold values from -0.09375 to 0.09375
Outputs:
- attended: bfloat16 [8, 512, 2048], P('dp', 'ctx')
- grad_queries: bfloat16 [8, 512, 2048], P('dp', 'ctx')
- grad_tokens: bfloat16 [8, 512, 4096], P('dp', 'ctx')
- grad_key_weight: float32 [4096, 512], P(('ctx', 'dp'))
- grad_value_weight: float32 [4096, 512], P(('ctx', 'dp'))
- grad_gain: float32 [4096], P(('ctx', 'dp'))
The draws below stay inside these ranges and needn't reach their ends.
All inputs are finite; a program needn't handle non-finite values.
Results may differ from the reference program's by a relative error of at most 0.025.
The reference program's roundings to bfloat16 on the way (of `normed`, `rotated_keys`, `value_rows`, `probability_b`, `dscores`, `key_pre_grad` and `value_pre_grad`) count: a program that leaves them out, or rounds other values in their place, can miss the bound.
Values may be sent and summed in bfloat16 or wider, within the bound.
No kernel may reach another device: no remote copies, remote signals or barrier semaphores. Data moves between devices by JAX's collectives and lax.ppermute only.
A program may use at most 192 MiB of HBM per device.

```python
import jax
import jax.numpy as jnp
from jax import lax

D = 4096
HEADS = 16
KV_HEADS = 4
HEAD_DIM = 128
SEQ_DEV = 64
SEQ = 512
SEQS = 8
N_CTX = 8


def draw_queries(key, part):
    full_shape = (SEQS, SEQ, HEADS * HEAD_DIM)
    sample = jnp.clip(jax.random.normal(key, full_shape, jnp.float32), -4.0, 4.0)
    return sample.astype(jnp.bfloat16)


def shard_levels(own_key, extent, shards, smallest, largest):
    factor_of = 1.0
    for axis_at, parts in shards:
        heights = jax.random.uniform(jax.random.fold_in(jax.random.fold_in(own_key, 6), axis_at), (parts,), jnp.float32, smallest / len(shards), largest / len(shards))
        factor_of = factor_of * jnp.repeat(jnp.exp(heights), extent[axis_at] // parts).reshape((-1,) + (1,) * (len(extent) - 1 - axis_at))
    return factor_of


def gaussian(key, shape, scale, limit, shards=(), kind=jnp.bfloat16):
    factor_of = shard_levels(key, shape, shards, -0.22, 0.18) if shards else 1.0
    entries = jax.random.normal(key, shape, jnp.float32) * scale * factor_of
    return jnp.minimum(jnp.maximum(entries, -limit), limit).astype(kind)


def setup_inputs(seed: int = 0) -> dict:
    arg_keys = jax.random.split(jax.random.key(seed), 8)
    return {
        "tokens": gaussian(arg_keys[0], (SEQS, SEQ, D), 1.0, 6.0, ((0, 4), (1, 8))),
        "queries": draw_queries(jax.random.fold_in(arg_keys[7], 71), 0),
        "d_attended": gaussian(arg_keys[2], (SEQS, SEQ, HEADS * HEAD_DIM), 1.0, 6.0, ((0, 4), (1, 8))),
        "span_order": jax.random.permutation(arg_keys[3], 2 * N_CTX).astype(jnp.int32),
        "norm_gain": jnp.clip(1.0 + 0.18 * jax.random.normal(arg_keys[4], (D,), jnp.float32), 0.1, 1.9),
        "key_weight": gaussian(arg_keys[5], (D, KV_HEADS * HEAD_DIM), D ** -0.5, 0.09375),
        "value_weight": gaussian(arg_keys[6], (D, KV_HEADS * HEAD_DIM), D ** -0.5, 0.09375),
    }


ROPE_BASE = 500000.0
EPSILON = 1e-05

def positions(span_order, span_len):
    offsets = jnp.arange(span_len, dtype=jnp.int32)
    return (span_order[:, None] * span_len + offsets[None, :]).reshape(-1).astype(jnp.int32)

def rotation(token_pos, head_size):
    half_dim = head_size // 2
    frequency = ROPE_BASE ** (-2.0 * jnp.arange(half_dim, dtype=jnp.float32) / head_size)
    angles = token_pos.astype(jnp.float32)[:, None] * frequency[None, :]
    angles = jnp.concatenate([angles, angles], axis=1)
    return (jnp.cos(angles), jnp.sin(angles))

def rotate_half(values):
    half_dim = values.shape[-1] // 2
    return jnp.concatenate([-values[..., half_dim:], values[..., :half_dim]], axis=-1)

def rotate_back(values):
    half_dim = values.shape[-1] // 2
    return jnp.concatenate([values[..., half_dim:], -values[..., :half_dim]], axis=-1)

def normalize(tokens, norm_gain):
    widened = tokens.astype(jnp.float32)
    rms_scale = lax.rsqrt(lax.optimization_barrier(jnp.mean(widened * widened, axis=-1, keepdims=True)) + EPSILON)
    return ((widened * rms_scale * norm_gain).astype(jnp.bfloat16), rms_scale)

def project_keys(normed, key_weight, value_weight, cosine, sine_table, kv_heads, head_size):
    row_count = normed.shape[0]
    key_pre = jnp.dot(normed, key_weight, preferred_element_type=jnp.float32).reshape(row_count, kv_heads, head_size)
    rotated = key_pre * cosine[:, None, :] + rotate_half(key_pre) * sine_table[:, None, :]
    value_rows = jnp.dot(normed, value_weight, preferred_element_type=jnp.float32)
    return (rotated.reshape(row_count, kv_heads * head_size).astype(jnp.bfloat16), value_rows.astype(jnp.bfloat16))

def attend_group(query_group, grad_group, key_group, value_group, causal_mask, score_scale):
    query_wide = query_group.astype(jnp.float32)
    grad_wide = grad_group.astype(jnp.float32)
    key_wide = key_group.astype(jnp.float32)
    value_wide = value_group.astype(jnp.float32)
    scores = jnp.einsum('tgd,sd->gts', query_wide, key_wide) * score_scale
    scores = jnp.where(causal_mask[None], scores, -1e+30)
    row_max = lax.optimization_barrier(jnp.max(scores, axis=-1, keepdims=True))
    exponent = jnp.exp(scores - row_max)
    probability = exponent / lax.optimization_barrier(jnp.sum(exponent, axis=-1, keepdims=True))
    probability_b = probability.astype(jnp.bfloat16)
    prob_wide = probability_b.astype(jnp.float32)
    attended = jnp.einsum('gts,sd->tgd', prob_wide, value_wide).astype(jnp.bfloat16)
    dprob = jnp.einsum('tgd,sd->gts', grad_wide, value_wide)
    delta = lax.optimization_barrier(jnp.sum(grad_wide * attended.astype(jnp.float32), axis=-1))
    dscores = (probability * (dprob - jnp.transpose(delta)[:, :, None])).astype(jnp.bfloat16)
    dscore_wide = dscores.astype(jnp.float32)
    dquery = (jnp.einsum('gts,sd->tgd', dscore_wide, key_wide) * score_scale).astype(jnp.bfloat16)
    key_term = jnp.einsum('gts,tgd->sd', dscore_wide, query_wide) * score_scale
    value_term = jnp.einsum('gts,tgd->sd', prob_wide, grad_wide)
    return (attended, dquery, key_term, value_term)

def attend_device(queries, grads, all_keys, all_values, query_pos, key_pos, kv_heads, head_size):
    row_count = queries.shape[0]
    group_size = queries.shape[1] // (kv_heads * head_size)
    group_width = group_size * head_size
    causal_mask = key_pos[None, :] <= query_pos[:, None]
    score_scale = head_size ** (-0.5)
    outputs = []
    for head_group in range(kv_heads):
        query_group = queries[:, head_group * group_width:(head_group + 1) * group_width].reshape(row_count, group_size, head_size)
        grad_group = grads[:, head_group * group_width:(head_group + 1) * group_width].reshape(row_count, group_size, head_size)
        key_group = all_keys[:, head_group * head_size:(head_group + 1) * head_size]
        value_group = all_values[:, head_group * head_size:(head_group + 1) * head_size]
        outputs.append(attend_group(query_group, grad_group, key_group, value_group, causal_mask, score_scale))
    attended = jnp.concatenate([item[0].reshape(row_count, group_width) for item in outputs], axis=1)
    dquery = jnp.concatenate([item[1].reshape(row_count, group_width) for item in outputs], axis=1)
    key_terms = jnp.concatenate([item[2] for item in outputs], axis=1)
    value_terms = jnp.concatenate([item[3] for item in outputs], axis=1)
    return (attended, dquery, key_terms, value_terms)

def finish_backward(tokens, normed, rms_scale, key_grad, value_grad, cosine, sine_table, norm_gain, key_weight, value_weight, kv_heads, head_size):
    row_count = tokens.shape[0]
    shaped = key_grad.reshape(row_count, kv_heads, head_size)
    key_pre_grad = (shaped * cosine[:, None, :] + rotate_back(shaped * sine_table[:, None, :])).reshape(row_count, kv_heads * head_size).astype(jnp.bfloat16)
    value_pre_grad = value_grad.astype(jnp.bfloat16)
    weight_key = jnp.dot(normed.T, key_pre_grad, preferred_element_type=jnp.float32)
    weight_value = jnp.dot(normed.T, value_pre_grad, preferred_element_type=jnp.float32)
    normed_grad = jnp.dot(key_pre_grad, key_weight.T, preferred_element_type=jnp.float32) + jnp.dot(value_pre_grad, value_weight.T, preferred_element_type=jnp.float32)
    widened = tokens.astype(jnp.float32)
    gain_part = lax.optimization_barrier(jnp.sum(normed_grad * widened * rms_scale, axis=0))
    inner_mean = lax.optimization_barrier(jnp.mean(normed_grad * norm_gain * widened, axis=-1, keepdims=True))
    grad_rows = (rms_scale * norm_gain * normed_grad - widened * rms_scale ** 3 * inner_mean).astype(jnp.bfloat16)
    return (grad_rows, weight_key, weight_value, gain_part)

def reference(tokens, queries, d_attended, span_order, norm_gain, key_weight, value_weight):
    token_pos = positions(span_order, SEQ_DEV // 2)
    cosine, sine_table = rotation(token_pos, HEAD_DIM)
    kv_width = KV_HEADS * HEAD_DIM
    total_key = jnp.zeros((D, kv_width), jnp.float32)
    total_value = jnp.zeros((D, kv_width), jnp.float32)
    total_gain = jnp.zeros((D,), jnp.float32)
    attended_list, dquery_list, dtoken_list = ([], [], [])
    for sequence in range(SEQS):
        normed, rms_scale = normalize(tokens[sequence], norm_gain)
        rotated_keys, value_rows = project_keys(normed, key_weight, value_weight, cosine, sine_table, KV_HEADS, HEAD_DIM)
        seq_queries = queries[sequence]
        seq_grads = d_attended[sequence]

        def shard_step(totals, shard_index):
            first_row = shard_index * SEQ_DEV
            block_queries = lax.dynamic_slice_in_dim(seq_queries, first_row, SEQ_DEV, 0)
            block_grads = lax.dynamic_slice_in_dim(seq_grads, first_row, SEQ_DEV, 0)
            query_pos = lax.dynamic_slice_in_dim(token_pos, first_row, SEQ_DEV, 0)
            attended, dquery, key_terms, value_terms = attend_device(block_queries, block_grads, rotated_keys, value_rows, query_pos, token_pos, KV_HEADS, HEAD_DIM)
            key_round = lax.optimization_barrier(key_terms.astype(jnp.bfloat16)).astype(jnp.float32)
            value_round = lax.optimization_barrier(value_terms.astype(jnp.bfloat16)).astype(jnp.float32)
            return ((totals[0] + key_round, totals[1] + value_round), (attended, dquery))
        zeros_init = jnp.zeros((SEQ, kv_width), jnp.float32)
        sums, stacked = lax.scan(shard_step, (zeros_init, zeros_init), jnp.arange(N_CTX, dtype=jnp.int32))
        attended_list.append(stacked[0].reshape(SEQ, HEADS * HEAD_DIM))
        dquery_list.append(stacked[1].reshape(SEQ, HEADS * HEAD_DIM))
        grad_rows, weight_key, weight_value, gain_part = finish_backward(tokens[sequence], normed, rms_scale, sums[0], sums[1], cosine, sine_table, norm_gain, key_weight, value_weight, KV_HEADS, HEAD_DIM)
        dtoken_list.append(grad_rows)
        total_key = total_key + weight_key
        total_value = total_value + weight_value
        total_gain = total_gain + gain_part
    return (jnp.stack(attended_list), jnp.stack(dquery_list), jnp.stack(dtoken_list), total_key, total_value, total_gain)
```

```python
import jax
import jax.numpy as jnp
from jax import lax
from jax.experimental import pallas as pl
from jax.experimental.pallas import tpu as pltpu
from jax.sharding import PartitionSpec as P

KV_HEADS = 4
HEAD_DIM = 128


ROPE_BASE = 500000.0
EPSILON = 1e-05


def positions(span_order, span_len):
    offsets = jnp.arange(span_len, dtype=jnp.int32)
    return (span_order[:, None] * span_len + offsets[None, :]).reshape(-1)


def rotation(token_pos, head_size):
    half_dim = head_size // 2
    frequency = ROPE_BASE ** (-2.0 * jnp.arange(half_dim, dtype=jnp.float32) / head_size)
    angles = token_pos.astype(jnp.float32)[:, None] * frequency[None, :]
    angles = jnp.concatenate([angles, angles], axis=1)
    return (jnp.cos(angles), jnp.sin(angles))


def rotate_half(values):
    half_dim = values.shape[-1] // 2
    return jnp.concatenate([-values[..., half_dim:], values[..., :half_dim]], axis=-1)


def rotate_back(values):
    half_dim = values.shape[-1] // 2
    return jnp.concatenate([values[..., half_dim:], -values[..., :half_dim]], axis=-1)


def normalize(tokens, norm_gain):
    widened = tokens.astype(jnp.float32)
    rms_scale = lax.rsqrt(jnp.mean(widened * widened, axis=-1, keepdims=True) + EPSILON)
    return ((widened * rms_scale * norm_gain).astype(jnp.bfloat16), rms_scale)


def project_keys(normed, key_weight, value_weight, cosine, sine_table, kv_heads, head_size):
    row_count = normed.shape[0]
    key_pre = jnp.dot(normed, key_weight, preferred_element_type=jnp.float32).reshape(
        row_count, kv_heads, head_size
    )
    rotated = key_pre * cosine[:, None, :] + rotate_half(key_pre) * sine_table[:, None, :]
    value_rows = jnp.dot(normed, value_weight, preferred_element_type=jnp.float32)
    return (
        rotated.reshape(row_count, kv_heads * head_size).astype(jnp.bfloat16),
        value_rows.astype(jnp.bfloat16),
    )


def attend_group(query_group, grad_group, key_group, value_group, causal_mask, score_scale):
    scores = (
        jnp.einsum("tgd,sd->gts", query_group, key_group, preferred_element_type=jnp.float32)
        * score_scale
    )
    scores = jnp.where(causal_mask[None], scores, -1e30)
    row_max = jnp.max(scores, axis=-1, keepdims=True)
    exponent = jnp.exp(scores - row_max)
    probability = exponent / jnp.sum(exponent, axis=-1, keepdims=True)
    probability_b = probability.astype(jnp.bfloat16)
    attended = jnp.einsum(
        "gts,sd->tgd", probability_b, value_group, preferred_element_type=jnp.float32
    ).astype(jnp.bfloat16)
    dprob = jnp.einsum("tgd,sd->gts", grad_group, value_group, preferred_element_type=jnp.float32)
    delta = jnp.sum(grad_group.astype(jnp.float32) * attended.astype(jnp.float32), axis=-1)
    dscores = (probability * (dprob - jnp.transpose(delta)[:, :, None])).astype(jnp.bfloat16)
    dquery = (
        jnp.einsum("gts,sd->tgd", dscores, key_group, preferred_element_type=jnp.float32)
        * score_scale
    ).astype(jnp.bfloat16)
    key_term = (
        jnp.einsum("gts,tgd->sd", dscores, query_group, preferred_element_type=jnp.float32)
        * score_scale
    )
    value_term = jnp.einsum(
        "gts,tgd->sd", probability_b, grad_group, preferred_element_type=jnp.float32
    )
    return (attended, dquery, key_term, value_term)


def attend_device(queries, grads, all_keys, all_values, query_pos, key_pos, kv_heads, head_size):
    row_count = queries.shape[0]
    group_size = queries.shape[1] // (kv_heads * head_size)
    group_width = group_size * head_size
    causal_mask = key_pos[None, :] <= query_pos[:, None]
    score_scale = head_size ** (-0.5)
    outputs = []
    for head_group in range(kv_heads):
        query_group = queries[:, head_group * group_width : (head_group + 1) * group_width].reshape(
            row_count, group_size, head_size
        )
        grad_group = grads[:, head_group * group_width : (head_group + 1) * group_width].reshape(
            row_count, group_size, head_size
        )
        key_group = all_keys[:, head_group * head_size : (head_group + 1) * head_size]
        value_group = all_values[:, head_group * head_size : (head_group + 1) * head_size]
        outputs.append(
            attend_group(query_group, grad_group, key_group, value_group, causal_mask, score_scale)
        )
    attended = jnp.concatenate(
        [item[0].reshape(row_count, group_width) for item in outputs], axis=1
    )
    dquery = jnp.concatenate([item[1].reshape(row_count, group_width) for item in outputs], axis=1)
    key_terms = jnp.concatenate([item[2] for item in outputs], axis=1)
    value_terms = jnp.concatenate([item[3] for item in outputs], axis=1)
    return (attended, dquery, key_terms, value_terms)


def finish_backward(
    tokens,
    normed,
    rms_scale,
    key_grad,
    value_grad,
    cosine,
    sine_table,
    norm_gain,
    key_weight,
    value_weight,
    kv_heads,
    head_size,
):
    row_count = tokens.shape[0]
    shaped = key_grad.reshape(row_count, kv_heads, head_size)
    key_pre_grad = (
        (shaped * cosine[:, None, :] + rotate_back(shaped * sine_table[:, None, :]))
        .reshape(row_count, kv_heads * head_size)
        .astype(jnp.bfloat16)
    )
    value_pre_grad = value_grad.astype(jnp.bfloat16)
    weight_key = jnp.dot(normed.T, key_pre_grad, preferred_element_type=jnp.float32)
    weight_value = jnp.dot(normed.T, value_pre_grad, preferred_element_type=jnp.float32)
    normed_grad = jnp.dot(key_pre_grad, key_weight.T, preferred_element_type=jnp.float32) + jnp.dot(
        value_pre_grad, value_weight.T, preferred_element_type=jnp.float32
    )
    widened = tokens.astype(jnp.float32)
    gain_part = jnp.sum(normed_grad * widened * rms_scale, axis=0)
    inner_mean = jnp.mean(normed_grad * norm_gain * widened, axis=-1, keepdims=True)
    grad_rows = (
        rms_scale * norm_gain * normed_grad - widened * rms_scale**3 * inner_mean
    ).astype(jnp.bfloat16)
    return (grad_rows, weight_key, weight_value, gain_part)


def body_rows(tokens, queries, d_attended, span_order, norm_gain, key_weight, value_weight):
    local_seqs = tokens.shape[0]
    row_count = tokens.shape[1]
    model_width = tokens.shape[2]
    kv_width = key_weight.shape[1]
    shard_index = lax.axis_index("ctx")
    token_pos = positions(span_order, row_count // 2)
    query_pos = lax.dynamic_slice_in_dim(token_pos, shard_index * row_count, row_count, 0)
    cosine, sine_table = rotation(query_pos, HEAD_DIM)
    cosine_all = jnp.tile(cosine, (local_seqs, 1))
    sine_all = jnp.tile(sine_table, (local_seqs, 1))
    flat_tokens = tokens.reshape(local_seqs * row_count, model_width)
    normed, rms_scale = normalize(flat_tokens, norm_gain)
    rotated_keys, value_rows = project_keys(
        normed, key_weight, value_weight, cosine_all, sine_all, KV_HEADS, HEAD_DIM
    )
    rotated_keys = rotated_keys.reshape(local_seqs, row_count, kv_width)
    value_rows = value_rows.reshape(local_seqs, row_count, kv_width)
    all_keys, all_values = (
        lax.all_gather(rotated_keys, "ctx", axis=1, tiled=True),
        lax.all_gather(value_rows, "ctx", axis=1, tiled=True),
    )
    attended_list, dquery_list, key_list, value_list = ([], [], [], [])
    for sequence in range(local_seqs):
        attended, dquery, key_terms, value_terms = attend_device(
            queries[sequence],
            d_attended[sequence],
            all_keys[sequence],
            all_values[sequence],
            query_pos,
            token_pos,
            KV_HEADS,
            HEAD_DIM,
        )
        attended_list.append(attended)
        dquery_list.append(dquery)
        key_list.append(key_terms)
        value_list.append(value_terms)
    key_stack = jnp.stack(key_list)
    value_stack = jnp.stack(value_list)
    key_grad, value_grad = (
        lax.psum_scatter(
            key_stack.astype(jnp.bfloat16), "ctx", scatter_dimension=1, tiled=True
        ).astype(jnp.float32),
        lax.psum_scatter(
            value_stack.astype(jnp.bfloat16), "ctx", scatter_dimension=1, tiled=True
        ).astype(jnp.float32),
    )
    key_grad = key_grad.reshape(local_seqs * row_count, kv_width)
    value_grad = value_grad.reshape(local_seqs * row_count, kv_width)
    grad_rows, weight_key, weight_value, gain_part = finish_backward(
        flat_tokens,
        normed,
        rms_scale,
        key_grad,
        value_grad,
        cosine_all,
        sine_all,
        norm_gain,
        key_weight,
        value_weight,
        KV_HEADS,
        HEAD_DIM,
    )
    weight_key, weight_value, gain_part = (
        lax.psum_scatter(
            weight_key.astype(jnp.bfloat16), "ctx", scatter_dimension=0, tiled=True
        ).astype(jnp.float32),
        lax.psum_scatter(
            weight_value.astype(jnp.bfloat16), "ctx", scatter_dimension=0, tiled=True
        ).astype(jnp.float32),
        lax.psum_scatter(
            gain_part.astype(jnp.bfloat16), "ctx", scatter_dimension=0, tiled=True
        ).astype(jnp.float32),
    )
    weight_key, weight_value, gain_part = (
        lax.psum_scatter(
            weight_key.astype(jnp.bfloat16), "dp", scatter_dimension=0, tiled=True
        ).astype(jnp.float32),
        lax.psum_scatter(
            weight_value.astype(jnp.bfloat16), "dp", scatter_dimension=0, tiled=True
        ).astype(jnp.float32),
        lax.psum_scatter(
            gain_part.astype(jnp.bfloat16), "dp", scatter_dimension=0, tiled=True
        ).astype(jnp.float32),
    )
    return (
        jnp.stack(attended_list),
        jnp.stack(dquery_list),
        grad_rows.reshape(local_seqs, row_count, model_width),
        weight_key,
        weight_value,
        gain_part,
    )


NT = (((1,), (1,)), ((), ()))


def dot32(left, right):
    return jnp.dot(left, right, preferred_element_type=jnp.float32)


def project_kernel(
    tok_all, tok_part, gain, wk, wv, cosine, sine, normed_out, rms_out, kv_out, acc_k, acc_v, rms_s
):
    step = pl.program_id(0)
    pairs, seq_rows, pair_width = kv_out.shape
    head = pair_width // 2

    @pl.when(step == 0)
    def _():
        wide = tok_all[...].astype(jnp.float32)
        rms_s[...] = lax.rsqrt(jnp.mean(wide * wide, axis=-1, keepdims=True) + EPSILON)
        rms_out[...] = rms_s[...]
        acc_k[...] = jnp.zeros_like(acc_k)
        acc_v[...] = jnp.zeros_like(acc_v)

    normed = (tok_part[...].astype(jnp.float32) * rms_s[...] * gain[...]).astype(jnp.bfloat16)
    normed_out[0] = normed
    acc_k[...] += dot32(normed, wk[...])
    acc_v[...] += dot32(normed, wv[...])

    @pl.when(step == pl.num_programs(0) - 1)
    def _():
        kv_heads = acc_k.shape[1] // head
        for group in range(kv_heads):
            columns = slice(group * head, (group + 1) * head)
            key_pre = acc_k[:, columns]
            rotated = key_pre * cosine[...] - pltpu.roll(key_pre, head // 2, 1) * sine[...]
            rotated = rotated.astype(jnp.bfloat16)
            value = acc_v[:, columns].astype(jnp.bfloat16)
            for seq in range(pairs // kv_heads):
                rows = slice(seq * seq_rows, (seq + 1) * seq_rows)
                kv_out[seq * kv_heads + group, :, :head] = rotated[rows]
                kv_out[seq * kv_heads + group, :, head:] = value[rows]


def attend_kernel(
    query, grad, kv, cosine, sine, key_pos, query_pos, att_out, dq_out, pre_out, acc_k, acc_v
):
    step = pl.program_id(0)
    head = query.shape[1]
    scale = head ** (-0.5)

    @pl.when(step == 0)
    def _():
        acc_k[...] = jnp.zeros_like(acc_k)
        acc_v[...] = jnp.zeros_like(acc_v)

    q = query[...]
    g = grad[...]
    k = kv[:, :head]
    v = kv[:, head:]
    grad_t = g.T
    scores = lax.dot_general(k, q, NT, preferred_element_type=jnp.float32) * scale
    scores = jnp.where(key_pos[...] <= query_pos[...], scores, -1e30)
    exponent = jnp.exp(scores - jnp.max(scores, axis=0, keepdims=True))
    prob = exponent * (1.0 / jnp.sum(exponent, axis=0, keepdims=True))
    prob_b = prob.astype(jnp.bfloat16)
    att_t = dot32(v.T, prob_b)
    att_out[...] = att_t.T.astype(jnp.bfloat16)
    att_r = att_t.astype(jnp.bfloat16).astype(jnp.float32)
    delta = jnp.sum(att_r * grad_t.astype(jnp.float32), axis=0, keepdims=True)
    dprob = dot32(v, grad_t)
    dscores = (prob * (dprob - delta)).astype(jnp.bfloat16)
    dq_out[...] = (dot32(k.T, dscores) * scale).T.astype(jnp.bfloat16)
    acc_k[...] += dot32(dscores, q)
    acc_v[...] += dot32(prob_b, g)

    @pl.when(step == pl.num_programs(0) - 1)
    def _():
        key_grad = acc_k[...] * scale
        back = key_grad * cosine[...] + pltpu.roll(key_grad, head // 2, 1) * sine[...]
        pre_out[:, :head] = back.astype(jnp.bfloat16)
        pre_out[:, head:] = acc_v[...].astype(jnp.bfloat16)


def weight_kernel(normed_t, pre, out):
    seqs, _, seq, _ = pre.shape
    total = dot32(normed_t[:, :seq], pre[0, 0])
    for s in range(1, seqs):
        total += dot32(normed_t[:, s * seq : (s + 1) * seq], pre[s, 0])
    out[...] = total.astype(jnp.bfloat16).reshape(out.shape)


def token_kernel(place, pre, wk, wv, tok_all, tok_part, gain, gain_part, rms, out, pk, pv, ng, inner):
    step = pl.program_id(0)
    seqs, kv_heads, _, rows, pair_width = pre.shape
    head = pair_width // 2

    @pl.when(step == 0)
    def _():
        for s in range(seqs):
            for h in range(kv_heads):
                pk[s * rows : (s + 1) * rows, h * head : (h + 1) * head] = pre[s, h, 0, :, :head]
                pv[s * rows : (s + 1) * rows, h * head : (h + 1) * head] = pre[s, h, 0, :, head:]
        inner[...] = jnp.zeros_like(inner)

    grad = lax.dot_general(pk[...], wk[...], NT, preferred_element_type=jnp.float32)
    grad += lax.dot_general(pv[...], wv[...], NT, preferred_element_type=jnp.float32)
    grad = grad * gain_part[...]
    ng[step] = grad
    inner[...] += jnp.sum(grad * tok_part[...].astype(jnp.float32), axis=-1, keepdims=True)

    @pl.when(step == pl.num_programs(0) - 1)
    def _():
        scale = rms[...]
        factor = scale * scale * scale * (inner[...] / tok_all.shape[1])
        width = ng.shape[2]
        for j in range(ng.shape[0]):
            part = slice(j * width, (j + 1) * width)
            wide = tok_all[:, part].astype(jnp.float32)
            out[:, part] = (scale * ng[j] - wide * factor).astype(jnp.bfloat16)


def last_kernel(place, parts, wk, wv, gk, gv, gain):
    total = parts[0].astype(jnp.float32)
    for i in range(1, parts.shape[0]):
        total += parts[i].astype(jnp.float32)
    kv_width = gk.shape[1]
    head = HEAD_DIM
    gain_sum = jnp.zeros((gk.shape[0], head), jnp.float32)
    for h in range(kv_width // head):
        columns = slice(h * head, (h + 1) * head)
        key_part = total[:, 2 * h * head : (2 * h + 1) * head]
        value_part = total[:, (2 * h + 1) * head : (2 * h + 2) * head]
        gk[:, columns] = key_part
        gv[:, columns] = value_part
        gain_sum += key_part * wk[:, columns].astype(jnp.float32)
        gain_sum += value_part * wv[:, columns].astype(jnp.float32)
    gain[...] = jnp.sum(gain_sum, axis=-1, keepdims=True)


def shape(dims, kind):
    return jax.ShapeDtypeStruct(dims, kind)


def whole_block(dims):
    return pl.BlockSpec(dims, lambda *_: (0,) * len(dims))


def exchange(values, axis):
    return lax.all_to_all(values, axis, split_axis=0, concat_axis=0, tiled=True)


def gather_ctx(values, count):
    copies = jnp.broadcast_to(values[None], (count,) + values.shape)
    return exchange(copies, "ctx")


def body_heads(tokens, queries, d_attended, span_order, norm_gain, key_weight, value_weight):
    bf16, f32 = jnp.bfloat16, jnp.float32
    seqs, rows, width = tokens.shape
    kv_width = key_weight.shape[1]
    kv_heads = kv_width // HEAD_DIM
    n_ctx = lax.axis_size("ctx")
    n_dp = lax.axis_size("dp")
    pairs = seqs * kv_heads
    seq = rows * n_ctx
    group_width = queries.shape[2] // kv_heads
    heads = group_width // HEAD_DIM
    part = width // n_ctx
    all_rows = seqs * rows
    pair_width = 2 * HEAD_DIM
    place = lax.axis_index("ctx").astype(jnp.int32)
    slot = (place * n_dp + lax.axis_index("dp").astype(jnp.int32)).reshape(1)

    def to_pairs(x):
        x = x.reshape(seqs, rows, kv_heads, group_width)
        return jnp.transpose(x, (0, 2, 1, 3)).reshape(pairs, rows, group_width)

    def from_pairs(x):
        x = x.reshape(seqs, kv_heads, rows, group_width)
        return jnp.transpose(x, (0, 2, 1, 3)).reshape(seqs, rows, kv_heads * group_width)

    q_in = exchange(to_pairs(queries), "ctx").reshape(seq, group_width)
    g_in = exchange(to_pairs(d_attended), "ctx").reshape(seq, group_width)

    token_pos = positions(span_order, rows // 2)
    cosine, sine = rotation(token_pos, HEAD_DIM)
    sign = jnp.where(jnp.arange(HEAD_DIM) < HEAD_DIM // 2, 1.0, -1.0).astype(f32)
    sine = sine * sign[None, :]
    own_cos = jnp.tile(lax.dynamic_slice_in_dim(cosine, place * rows, rows, 0), (seqs, 1))
    own_sin = jnp.tile(lax.dynamic_slice_in_dim(sine, place * rows, rows, 0), (seqs, 1))
    flat = tokens.reshape(all_rows, width)
    gain_row = norm_gain[None, :]

    normed, rms, kv = pl.pallas_call(
        project_kernel,
        grid=(n_ctx,),
        in_specs=[
            whole_block((all_rows, width)),
            pl.BlockSpec((all_rows, part), lambda j: (0, j)),
            pl.BlockSpec((1, part), lambda j: (0, j)),
            pl.BlockSpec((part, kv_width), lambda j: (j, 0)),
            pl.BlockSpec((part, kv_width), lambda j: (j, 0)),
            whole_block((all_rows, HEAD_DIM)),
            whole_block((all_rows, HEAD_DIM)),
        ],
        out_specs=[
            pl.BlockSpec((1, all_rows, part), lambda j: (j, 0, 0)),
            whole_block((all_rows, 1)),
            whole_block((pairs, rows, pair_width)),
        ],
        out_shape=[
            shape((n_ctx, all_rows, part), bf16),
            shape((all_rows, 1), f32),
            shape((pairs, rows, pair_width), bf16),
        ],
        scratch_shapes=[
            pltpu.VMEM((all_rows, kv_width), f32),
            pltpu.VMEM((all_rows, kv_width), f32),
            pltpu.VMEM((all_rows, 1), f32),
        ],
        name="project",
    )(flat, flat, gain_row, key_weight, value_weight, own_cos, own_sin)

    kv_in = exchange(kv, "ctx").reshape(seq, pair_width)
    normed_in = exchange(normed, "ctx").reshape(n_ctx, seqs, rows, part)
    normed_t = jnp.transpose(normed_in, (3, 1, 0, 2)).reshape(part, seqs * seq)

    attended, dquery, pre = pl.pallas_call(
        attend_kernel,
        grid=(heads,),
        in_specs=[
            pl.BlockSpec((seq, HEAD_DIM), lambda h: (0, h)),
            pl.BlockSpec((seq, HEAD_DIM), lambda h: (0, h)),
            whole_block((seq, pair_width)),
            whole_block((seq, HEAD_DIM)),
            whole_block((seq, HEAD_DIM)),
            whole_block((seq, 1)),
            whole_block((1, seq)),
        ],
        out_specs=[
            pl.BlockSpec((seq, HEAD_DIM), lambda h: (0, h)),
            pl.BlockSpec((seq, HEAD_DIM), lambda h: (0, h)),
            whole_block((seq, pair_width)),
        ],
        out_shape=[
            shape((seq, group_width), bf16),
            shape((seq, group_width), bf16),
            shape((seq, pair_width), bf16),
        ],
        scratch_shapes=[pltpu.VMEM((seq, HEAD_DIM), f32), pltpu.VMEM((seq, HEAD_DIM), f32)],
        name="attend",
    )(q_in, g_in, kv_in, cosine, sine, token_pos[:, None], token_pos[None, :])

    pre_all = gather_ctx(pre, n_ctx).reshape(seqs, kv_heads, seq, pair_width)

    weight_parts = pl.pallas_call(
        weight_kernel,
        grid=(kv_heads,),
        in_specs=[
            whole_block((part, seqs * seq)),
            pl.BlockSpec((seqs, 1, seq, pair_width), lambda h: (0, h, 0, 0)),
        ],
        out_specs=pl.BlockSpec((n_dp, part // n_dp, pair_width), lambda h: (0, 0, h)),
        out_shape=shape((n_dp, part // n_dp, 2 * kv_width), bf16),
        name="weights",
    )(normed_t, pre_all)
    weight_in = exchange(weight_parts, "dp")

    att_back = from_pairs(exchange(attended.reshape(n_ctx, rows, group_width), "ctx"))
    dq_back = from_pairs(exchange(dquery.reshape(n_ctx, rows, group_width), "ctx"))

    grad_tokens = pl.pallas_call(
        token_kernel,
        grid_spec=pltpu.PrefetchScalarGridSpec(
            num_scalar_prefetch=1,
            grid=(n_ctx,),
            in_specs=[
                pl.BlockSpec((seqs, kv_heads, 1, rows, pair_width), lambda j, p: (0, 0, p[0], 0, 0)),
                pl.BlockSpec((part, kv_width), lambda j, p: (j, 0)),
                pl.BlockSpec((part, kv_width), lambda j, p: (j, 0)),
                whole_block((all_rows, width)),
                pl.BlockSpec((all_rows, part), lambda j, p: (0, j)),
                whole_block((1, width)),
                pl.BlockSpec((1, part), lambda j, p: (0, j)),
                whole_block((all_rows, 1)),
            ],
            out_specs=whole_block((all_rows, width)),
            scratch_shapes=[
                pltpu.VMEM((all_rows, kv_width), bf16),
                pltpu.VMEM((all_rows, kv_width), bf16),
                pltpu.VMEM((n_ctx, all_rows, part), f32),
                pltpu.VMEM((all_rows, 1), f32),
            ],
        ),
        out_shape=shape((all_rows, width), bf16),
        name="tokens",
    )(
        place.reshape(1),
        pre_all.reshape(seqs, kv_heads, n_ctx, rows, pair_width),
        key_weight,
        value_weight,
        flat,
        flat,
        gain_row,
        gain_row,
        rms,
    )

    own = part // n_dp
    grad_key, grad_value, gain_sum = pl.pallas_call(
        last_kernel,
        grid_spec=pltpu.PrefetchScalarGridSpec(
            num_scalar_prefetch=1,
            grid=(1,),
            in_specs=[
                whole_block((n_dp, own, 2 * kv_width)),
                pl.BlockSpec((own, kv_width), lambda j, p: (p[0], 0)),
                pl.BlockSpec((own, kv_width), lambda j, p: (p[0], 0)),
            ],
            out_specs=[
                whole_block((own, kv_width)),
                whole_block((own, kv_width)),
                whole_block((own, 1)),
            ],
        ),
        out_shape=[shape((own, kv_width), f32), shape((own, kv_width), f32), shape((own, 1), f32)],
        name="last",
    )(slot, weight_in, key_weight, value_weight)
    own_gain = lax.dynamic_slice_in_dim(norm_gain, slot[0] * own, own, 0)
    grad_gain = gain_sum[:, 0] / own_gain
    return (
        att_back,
        dq_back,
        grad_tokens.reshape(seqs, rows, width),
        grad_key,
        grad_value,
        grad_gain,
    )


def body(tokens, queries, d_attended, span_order, norm_gain, key_weight, value_weight):
    pairs = tokens.shape[0] * (key_weight.shape[1] // HEAD_DIM)
    chosen = body_heads if pairs == lax.axis_size("ctx") else body_rows
    return chosen(tokens, queries, d_attended, span_order, norm_gain, key_weight, value_weight)


def solution(mesh):
    placed = (P("dp", "ctx", None), P("dp", "ctx", None), P("dp", "ctx", None), P(), P(), P(), P())
    return jax.shard_map(
        body,
        mesh=mesh,
        in_specs=placed,
        out_specs=(
            P("dp", "ctx", None),
            P("dp", "ctx", None),
            P("dp", "ctx", None),
            P(("ctx", "dp"), None),
            P(("ctx", "dp"), None),
            P(("ctx", "dp")),
        ),
        check_vma=False,
    )
```

```python
import jax
import jax.numpy as jnp
from jax import lax
from jax.experimental import pallas as pl
from jax.experimental.pallas import tpu as pltpu
from jax.sharding import PartitionSpec as P


KV_HEADS = 4
HEAD_DIM = 128


ROPE_BASE = 500000.0
EPSILON = 1e-05


def positions(span_order, span_len):
    offsets = jnp.arange(span_len, dtype=jnp.int32)
    return (span_order[:, None] * span_len + offsets[None, :]).reshape(-1)


def rotation(token_pos, head_size):
    half_dim = head_size // 2
    frequency = ROPE_BASE ** (-2.0 * jnp.arange(half_dim, dtype=jnp.float32) / head_size)
    angles = token_pos.astype(jnp.float32)[:, None] * frequency[None, :]
    angles = jnp.concatenate([angles, angles], axis=1)
    return (jnp.cos(angles), jnp.sin(angles))


def rotate_half(values):
    half_dim = values.shape[-1] // 2
    return jnp.concatenate([-values[..., half_dim:], values[..., :half_dim]], axis=-1)


def rotate_back(values):
    half_dim = values.shape[-1] // 2
    return jnp.concatenate([values[..., half_dim:], -values[..., :half_dim]], axis=-1)


def normalize(tokens, norm_gain):
    widened = tokens.astype(jnp.float32)
    rms_scale = lax.rsqrt(jnp.mean(widened * widened, axis=-1, keepdims=True) + EPSILON)
    return ((widened * rms_scale * norm_gain).astype(jnp.bfloat16), rms_scale)


def project_keys(normed, key_weight, value_weight, cosine, sine_table, kv_heads, head_size):
    row_count = normed.shape[0]
    key_pre = jnp.dot(normed, key_weight, preferred_element_type=jnp.float32).reshape(
        row_count, kv_heads, head_size
    )
    rotated = key_pre * cosine[:, None, :] + rotate_half(key_pre) * sine_table[:, None, :]
    value_rows = jnp.dot(normed, value_weight, preferred_element_type=jnp.float32)
    return (
        rotated.reshape(row_count, kv_heads * head_size).astype(jnp.bfloat16),
        value_rows.astype(jnp.bfloat16),
    )


def attend_group(query_group, grad_group, key_group, value_group, causal_mask, score_scale):
    scores = (
        jnp.einsum("tgd,sd->gts", query_group, key_group, preferred_element_type=jnp.float32)
        * score_scale
    )
    scores = jnp.where(causal_mask[None], scores, -1e30)
    row_max = jnp.max(scores, axis=-1, keepdims=True)
    exponent = jnp.exp(scores - row_max)
    probability = exponent / jnp.sum(exponent, axis=-1, keepdims=True)
    probability_b = probability.astype(jnp.bfloat16)
    attended = jnp.einsum(
        "gts,sd->tgd", probability_b, value_group, preferred_element_type=jnp.float32
    ).astype(jnp.bfloat16)
    dprob = jnp.einsum("tgd,sd->gts", grad_group, value_group, preferred_element_type=jnp.float32)
    delta = jnp.sum(grad_group.astype(jnp.float32) * attended.astype(jnp.float32), axis=-1)
    dscores = (probability * (dprob - jnp.transpose(delta)[:, :, None])).astype(jnp.bfloat16)
    dquery = (
        jnp.einsum("gts,sd->tgd", dscores, key_group, preferred_element_type=jnp.float32)
        * score_scale
    ).astype(jnp.bfloat16)
    key_term = (
        jnp.einsum("gts,tgd->sd", dscores, query_group, preferred_element_type=jnp.float32)
        * score_scale
    )
    value_term = jnp.einsum(
        "gts,tgd->sd", probability_b, grad_group, preferred_element_type=jnp.float32
    )
    return (attended, dquery, key_term, value_term)


def attend_device(queries, grads, all_keys, all_values, query_pos, key_pos, kv_heads, head_size):
    row_count = queries.shape[0]
    group_size = queries.shape[1] // (kv_heads * head_size)
    group_width = group_size * head_size
    causal_mask = key_pos[None, :] <= query_pos[:, None]
    score_scale = head_size ** (-0.5)
    outputs = []
    for head_group in range(kv_heads):
        query_group = queries[:, head_group * group_width : (head_group + 1) * group_width].reshape(
            row_count, group_size, head_size
        )
        grad_group = grads[:, head_group * group_width : (head_group + 1) * group_width].reshape(
            row_count, group_size, head_size
        )
        key_group = all_keys[:, head_group * head_size : (head_group + 1) * head_size]
        value_group = all_values[:, head_group * head_size : (head_group + 1) * head_size]
        outputs.append(
            attend_group(query_group, grad_group, key_group, value_group, causal_mask, score_scale)
        )
    attended = jnp.concatenate(
        [item[0].reshape(row_count, group_width) for item in outputs], axis=1
    )
    dquery = jnp.concatenate([item[1].reshape(row_count, group_width) for item in outputs], axis=1)
    key_terms = jnp.concatenate([item[2] for item in outputs], axis=1)
    value_terms = jnp.concatenate([item[3] for item in outputs], axis=1)
    return (attended, dquery, key_terms, value_terms)


def finish_backward(
    tokens,
    normed,
    rms_scale,
    key_grad,
    value_grad,
    cosine,
    sine_table,
    norm_gain,
    key_weight,
    value_weight,
    kv_heads,
    head_size,
):
    row_count = tokens.shape[0]
    shaped = key_grad.reshape(row_count, kv_heads, head_size)
    key_pre_grad = (
        (shaped * cosine[:, None, :] + rotate_back(shaped * sine_table[:, None, :]))
        .reshape(row_count, kv_heads * head_size)
        .astype(jnp.bfloat16)
    )
    value_pre_grad = value_grad.astype(jnp.bfloat16)
    weight_key = jnp.dot(normed.T, key_pre_grad, preferred_element_type=jnp.float32)
    weight_value = jnp.dot(normed.T, value_pre_grad, preferred_element_type=jnp.float32)
    normed_grad = jnp.dot(key_pre_grad, key_weight.T, preferred_element_type=jnp.float32) + jnp.dot(
        value_pre_grad, value_weight.T, preferred_element_type=jnp.float32
    )
    widened = tokens.astype(jnp.float32)
    gain_part = jnp.sum(normed_grad * widened * rms_scale, axis=0)
    inner_mean = jnp.mean(normed_grad * norm_gain * widened, axis=-1, keepdims=True)
    grad_rows = (
        rms_scale * norm_gain * normed_grad - widened * rms_scale**3 * inner_mean
    ).astype(jnp.bfloat16)
    return (grad_rows, weight_key, weight_value, gain_part)


def body_rows(tokens, queries, d_attended, span_order, norm_gain, key_weight, value_weight):
    local_seqs = tokens.shape[0]
    row_count = tokens.shape[1]
    model_width = tokens.shape[2]
    kv_width = key_weight.shape[1]
    shard_index = lax.axis_index("ctx")
    token_pos = positions(span_order, row_count // 2)
    query_pos = lax.dynamic_slice_in_dim(token_pos, shard_index * row_count, row_count, 0)
    cosine, sine_table = rotation(query_pos, HEAD_DIM)
    cosine_all = jnp.tile(cosine, (local_seqs, 1))
    sine_all = jnp.tile(sine_table, (local_seqs, 1))
    flat_tokens = tokens.reshape(local_seqs * row_count, model_width)
    normed, rms_scale = normalize(flat_tokens, norm_gain)
    rotated_keys, value_rows = project_keys(
        normed, key_weight, value_weight, cosine_all, sine_all, KV_HEADS, HEAD_DIM
    )
    rotated_keys = rotated_keys.reshape(local_seqs, row_count, kv_width)
    value_rows = value_rows.reshape(local_seqs, row_count, kv_width)
    all_keys, all_values = (
        lax.all_gather(rotated_keys, "ctx", axis=1, tiled=True),
        lax.all_gather(value_rows, "ctx", axis=1, tiled=True),
    )
    attended_list, dquery_list, key_list, value_list = ([], [], [], [])
    for sequence in range(local_seqs):
        attended, dquery, key_terms, value_terms = attend_device(
            queries[sequence],
            d_attended[sequence],
            all_keys[sequence],
            all_values[sequence],
            query_pos,
            token_pos,
            KV_HEADS,
            HEAD_DIM,
        )
        attended_list.append(attended)
        dquery_list.append(dquery)
        key_list.append(key_terms)
        value_list.append(value_terms)
    key_stack = jnp.stack(key_list)
    value_stack = jnp.stack(value_list)
    key_grad, value_grad = (
        lax.psum_scatter(
            key_stack.astype(jnp.bfloat16), "ctx", scatter_dimension=1, tiled=True
        ).astype(jnp.float32),
        lax.psum_scatter(
            value_stack.astype(jnp.bfloat16), "ctx", scatter_dimension=1, tiled=True
        ).astype(jnp.float32),
    )
    key_grad = key_grad.reshape(local_seqs * row_count, kv_width)
    value_grad = value_grad.reshape(local_seqs * row_count, kv_width)
    grad_rows, weight_key, weight_value, gain_part = finish_backward(
        flat_tokens,
        normed,
        rms_scale,
        key_grad,
        value_grad,
        cosine_all,
        sine_all,
        norm_gain,
        key_weight,
        value_weight,
        KV_HEADS,
        HEAD_DIM,
    )
    weight_key, weight_value, gain_part = (
        lax.psum_scatter(
            weight_key.astype(jnp.bfloat16), "ctx", scatter_dimension=0, tiled=True
        ).astype(jnp.float32),
        lax.psum_scatter(
            weight_value.astype(jnp.bfloat16), "ctx", scatter_dimension=0, tiled=True
        ).astype(jnp.float32),
        lax.psum_scatter(
            gain_part.astype(jnp.bfloat16), "ctx", scatter_dimension=0, tiled=True
        ).astype(jnp.float32),
    )
    weight_key, weight_value, gain_part = (
        lax.psum_scatter(
            weight_key.astype(jnp.bfloat16), "dp", scatter_dimension=0, tiled=True
        ).astype(jnp.float32),
        lax.psum_scatter(
            weight_value.astype(jnp.bfloat16), "dp", scatter_dimension=0, tiled=True
        ).astype(jnp.float32),
        lax.psum_scatter(
            gain_part.astype(jnp.bfloat16), "dp", scatter_dimension=0, tiled=True
        ).astype(jnp.float32),
    )
    return (
        jnp.stack(attended_list),
        jnp.stack(dquery_list),
        grad_rows.reshape(local_seqs, row_count, model_width),
        weight_key,
        weight_value,
        gain_part,
    )


NT = (((1,), (1,)), ((), ()))


def dot32(left, right):
    return jnp.dot(left, right, preferred_element_type=jnp.float32)


def project_kernel(
    place, tok_all, tok_part, gain, wk, wv, cosine, sine, normed_out, rms_out, kv_out, acc_k, acc_v, rms_s
):
    step = pl.program_id(0)
    pairs, seq_rows, pair_width = kv_out.shape
    head = pair_width // 2

    @pl.when(step == 0)
    def _():
        wide = tok_all[...].astype(jnp.float32)
        rms_s[...] = lax.rsqrt(jnp.mean(wide * wide, axis=-1, keepdims=True) + EPSILON)
        rms_out[...] = rms_s[...]
        acc_k[...] = jnp.zeros_like(acc_k)
        acc_v[...] = jnp.zeros_like(acc_v)

    normed = (tok_part[...].astype(jnp.float32) * rms_s[...] * gain[...]).astype(jnp.bfloat16)
    normed_out[0] = normed
    acc_k[...] += dot32(normed, wk[...])
    acc_v[...] += dot32(normed, wv[...])

    @pl.when(step == pl.num_programs(0) - 1)
    def _():
        kv_heads = acc_k.shape[1] // head
        for group in range(kv_heads):
            columns = slice(group * head, (group + 1) * head)
            key_pre = acc_k[:, columns]
            rotated = key_pre * cosine[...] - pltpu.roll(key_pre, head // 2, 1) * sine[...]
            rotated = rotated.astype(jnp.bfloat16)
            value = acc_v[:, columns].astype(jnp.bfloat16)
            for seq in range(pairs // kv_heads):
                rows = slice(seq * seq_rows, (seq + 1) * seq_rows)
                kv_out[seq * kv_heads + group, :, :head] = rotated[rows]
                kv_out[seq * kv_heads + group, :, head:] = value[rows]


def attend_kernel(
    query, grad, kv, cosine, sine, key_pos, query_pos, both_out, pre_out, acc_k, acc_v
):
    step = pl.program_id(0)
    head = query.shape[1]
    scale = head ** (-0.5)

    @pl.when(step == 0)
    def _():
        acc_k[...] = jnp.zeros_like(acc_k)
        acc_v[...] = jnp.zeros_like(acc_v)

    q = query[...]
    g = grad[...]
    k = kv[:, :head]
    v = kv[:, head:]
    grad_t = g.T
    scores = lax.dot_general(k, q, NT, preferred_element_type=jnp.float32) * scale
    scores = jnp.where(key_pos[...] <= query_pos[...], scores, -1e30)
    exponent = jnp.exp(scores - jnp.max(scores, axis=0, keepdims=True))
    prob = exponent * (1.0 / jnp.sum(exponent, axis=0, keepdims=True))
    prob_b = prob.astype(jnp.bfloat16)
    att_t = dot32(v.T, prob_b)
    both_out[:, :head] = att_t.T.astype(jnp.bfloat16)
    att_r = att_t.astype(jnp.bfloat16).astype(jnp.float32)
    delta = jnp.sum(att_r * grad_t.astype(jnp.float32), axis=0, keepdims=True)
    dprob = dot32(v, grad_t)
    dscores = (prob * (dprob - delta)).astype(jnp.bfloat16)
    both_out[:, head:] = (dot32(k.T, dscores) * scale).T.astype(jnp.bfloat16)
    acc_k[...] += dot32(dscores, q)
    acc_v[...] += dot32(prob_b, g)

    @pl.when(step == pl.num_programs(0) - 1)
    def _():
        key_grad = acc_k[...] * scale
        back = key_grad * cosine[...] + pltpu.roll(key_grad, head // 2, 1) * sine[...]
        pre_out[:, :head] = back.astype(jnp.bfloat16)
        pre_out[:, head:] = acc_v[...].astype(jnp.bfloat16)


def pack_kernel(query, grad, out):
    width = query.shape[2]
    out[0, :, :width] = query[0]
    out[0, :, width:] = grad[0]


def unpack_kernel(both, att, dq):
    for h in range(att.shape[2] // HEAD_DIM):
        columns = slice(h * HEAD_DIM, (h + 1) * HEAD_DIM)
        first = 2 * h * HEAD_DIM
        att[0, :, columns] = both[0, :, first : first + HEAD_DIM]
        dq[0, :, columns] = both[0, :, first + HEAD_DIM : first + 2 * HEAD_DIM]


def weight_kernel(place, *refs):
    *inputs, out, stacked, turned = refs
    seqs, seq, _ = stacked.shape
    pre, normed = inputs[:seqs], inputs[seqs:]
    rows = seq // len(normed)

    @pl.when(pl.program_id(0) == 0)
    def _():
        for s in range(seqs):
            for c, block in enumerate(normed):
                stacked[s, c * rows : (c + 1) * rows] = block[0, s]
            turned[s] = stacked[s].T

    total = dot32(turned[0], pre[0][0])
    for s in range(1, seqs):
        total += dot32(turned[s], pre[s][0])
    out[...] = total.astype(jnp.bfloat16).reshape(out.shape)


def token_kernel(place, *refs):
    *pre, wk, wv, tok_all, tok_part, gain_part, rms, out, pk, pv, ng, inner = refs
    step = pl.program_id(0)
    rows, pair_width = pre[0].shape[1:]
    head = pair_width // 2
    kv_heads = pk.shape[1] // head
    seqs = pk.shape[0] // rows

    @pl.when(step == 0)
    def _():
        for s in range(seqs):
            for h in range(kv_heads):
                pk[s * rows : (s + 1) * rows, h * head : (h + 1) * head] = pre[s * kv_heads + h][0, :, :head]
                pv[s * rows : (s + 1) * rows, h * head : (h + 1) * head] = pre[s * kv_heads + h][0, :, head:]
        inner[...] = jnp.zeros_like(inner)

    grad = lax.dot_general(pk[...], wk[...], NT, preferred_element_type=jnp.float32)
    grad += lax.dot_general(pv[...], wv[...], NT, preferred_element_type=jnp.float32)
    grad = grad * gain_part[...]
    ng[step] = grad
    inner[...] += jnp.sum(grad * tok_part[...].astype(jnp.float32), axis=-1, keepdims=True)

    @pl.when(step == pl.num_programs(0) - 1)
    def _():
        scale = rms[...]
        factor = scale * scale * scale * (inner[...] / tok_all.shape[1])
        width = ng.shape[2]
        for j in range(ng.shape[0]):
            part = slice(j * width, (j + 1) * width)
            wide = tok_all[:, part].astype(jnp.float32)
            out[:, part] = (scale * ng[j] - wide * factor).astype(jnp.bfloat16)


def last_kernel(place, parts, wk, wv, gk, gv, gain):
    total = parts[0].astype(jnp.float32)
    for i in range(1, parts.shape[0]):
        total += parts[i].astype(jnp.float32)
    kv_width = gk.shape[1]
    head = HEAD_DIM
    gain_sum = jnp.zeros((gk.shape[0], head), jnp.float32)
    for h in range(kv_width // head):
        columns = slice(h * head, (h + 1) * head)
        key_part = total[:, 2 * h * head : (2 * h + 1) * head]
        value_part = total[:, (2 * h + 1) * head : (2 * h + 2) * head]
        gk[:, columns] = key_part
        gv[:, columns] = value_part
        gain_sum += key_part * wk[:, columns].astype(jnp.float32)
        gain_sum += value_part * wv[:, columns].astype(jnp.float32)
    gain[...] = jnp.sum(gain_sum, axis=-1, keepdims=True)


def shape(dims, kind):
    return jax.ShapeDtypeStruct(dims, kind)


def whole_block(dims):
    return pl.BlockSpec(dims, lambda *_: (0,) * len(dims))


def exchange(values, axis):
    return lax.all_to_all(values, axis, split_axis=0, concat_axis=0, tiled=True)


def shifted(blocks):
    count = len(blocks)
    moved = [blocks[0]]
    for d in range(1, count):
        moved.append(lax.ppermute(blocks[d], "ctx", [(i, (i + d) % count) for i in range(count)]))
    return moved


def body_heads(tokens, queries, d_attended, span_order, norm_gain, key_weight, value_weight):
    bf16, f32 = jnp.bfloat16, jnp.float32
    seqs, rows, width = tokens.shape
    kv_width = key_weight.shape[1]
    kv_heads = kv_width // HEAD_DIM
    n_ctx = lax.axis_size("ctx")
    n_dp = lax.axis_size("dp")
    pairs = seqs * kv_heads
    seq = rows * n_ctx
    group_width = queries.shape[2] // kv_heads
    heads = group_width // HEAD_DIM
    part = width // n_ctx
    all_rows = seqs * rows
    pair_width = 2 * HEAD_DIM
    place = lax.axis_index("ctx").astype(jnp.int32)
    slot = (place * n_dp + lax.axis_index("dp").astype(jnp.int32)).reshape(1)

    own_block = pl.BlockSpec((1, rows, group_width), lambda i: (i // kv_heads, 0, i % kv_heads))
    pair_block = pl.BlockSpec((1, rows, 2 * group_width), lambda i: (i, 0, 0))
    both = pl.pallas_call(
        pack_kernel,
        grid=(pairs,),
        in_specs=[own_block, own_block],
        out_specs=pair_block,
        out_shape=shape((pairs, rows, 2 * group_width), bf16),
        name="pack",
    )(queries, d_attended)
    both_in = exchange(both, "ctx").reshape(seq, 2 * group_width)

    token_pos = positions(span_order, rows // 2)
    cosine, sine = rotation(token_pos, HEAD_DIM)
    sign = jnp.where(jnp.arange(HEAD_DIM) < HEAD_DIM // 2, 1.0, -1.0).astype(f32)
    sine = sine * sign[None, :]
    own_cos = jnp.tile(lax.dynamic_slice_in_dim(cosine, place * rows, rows, 0), (seqs, 1))
    own_sin = jnp.tile(lax.dynamic_slice_in_dim(sine, place * rows, rows, 0), (seqs, 1))
    flat = tokens.reshape(all_rows, width)
    gain_row = norm_gain[None, :]

    normed, rms, kv = pl.pallas_call(
        project_kernel,
        grid_spec=pltpu.PrefetchScalarGridSpec(
            num_scalar_prefetch=1,
            grid=(n_ctx,),
            in_specs=[
                whole_block((all_rows, width)),
                pl.BlockSpec((all_rows, part), lambda j, p: (0, j)),
                pl.BlockSpec((1, part), lambda j, p: (0, j)),
                pl.BlockSpec((part, kv_width), lambda j, p: (j, 0)),
                pl.BlockSpec((part, kv_width), lambda j, p: (j, 0)),
                whole_block((all_rows, HEAD_DIM)),
                whole_block((all_rows, HEAD_DIM)),
            ],
            out_specs=[
                pl.BlockSpec(
                    (1, all_rows, part), lambda j, p: (lax.rem(j - p[0] + n_ctx, n_ctx), 0, 0)
                ),
                whole_block((all_rows, 1)),
                whole_block((pairs, rows, pair_width)),
            ],
            scratch_shapes=[
                pltpu.VMEM((all_rows, kv_width), f32),
                pltpu.VMEM((all_rows, kv_width), f32),
                pltpu.VMEM((all_rows, 1), f32),
            ],
        ),
        out_shape=[
            shape((n_ctx, all_rows, part), bf16),
            shape((all_rows, 1), f32),
            shape((pairs, rows, pair_width), bf16),
        ],
        name="project",
    )(place.reshape(1), flat, flat, gain_row, key_weight, value_weight, own_cos, own_sin)

    kv_in = exchange(kv, "ctx").reshape(seq, pair_width)
    normed_in = shifted([normed[d] for d in range(n_ctx)])
    normed_in = [block.reshape(seqs, rows, part) for block in normed_in]
    normed_in = jnp.stack(normed_in)
    source = lax.rem(place - jnp.arange(n_ctx, dtype=jnp.int32) + n_ctx, n_ctx)
    source = jnp.concatenate([source, place.reshape(1)])

    both_out, pre = pl.pallas_call(
        attend_kernel,
        grid=(heads,),
        in_specs=[
            pl.BlockSpec((seq, HEAD_DIM), lambda h: (0, h)),
            pl.BlockSpec((seq, HEAD_DIM), lambda h: (0, heads + h)),
            whole_block((seq, pair_width)),
            whole_block((seq, HEAD_DIM)),
            whole_block((seq, HEAD_DIM)),
            whole_block((seq, 1)),
            whole_block((1, seq)),
        ],
        out_specs=[
            pl.BlockSpec((seq, pair_width), lambda h: (0, h)),
            whole_block((seq, pair_width)),
        ],
        out_shape=[
            shape((seq, 2 * group_width), bf16),
            shape((seq, pair_width), bf16),
        ],
        scratch_shapes=[pltpu.VMEM((seq, HEAD_DIM), f32), pltpu.VMEM((seq, HEAD_DIM), f32)],
        name="attend",
    )(both_in, both_in, kv_in, cosine, sine, token_pos[:, None], token_pos[None, :])

    pre_all = jnp.stack(shifted([pre] * n_ctx))

    weight_parts = pl.pallas_call(
        weight_kernel,
        grid_spec=pltpu.PrefetchScalarGridSpec(
            num_scalar_prefetch=1,
            grid=(kv_heads,),
            in_specs=[
                pl.BlockSpec((1, seq, pair_width), lambda h, p, s=s: (p[s * kv_heads + h], 0, 0))
                for s in range(seqs)
            ]
            + [
                pl.BlockSpec((1, seqs, rows, part), lambda h, p, c=c: (p[c], 0, 0, 0))
                for c in range(n_ctx)
            ],
            out_specs=pl.BlockSpec((n_dp, part // n_dp, pair_width), lambda h, p: (0, 0, h)),
            scratch_shapes=[
                pltpu.VMEM((seqs, seq, part), bf16),
                pltpu.VMEM((seqs, part, seq), bf16),
            ],
        ),
        out_shape=shape((n_dp, part // n_dp, 2 * kv_width), bf16),
        name="weights",
    )(source, *([pre_all] * seqs), *([normed_in] * n_ctx))
    weight_in = exchange(weight_parts, "dp")

    both_back = exchange(both_out.reshape(n_ctx, rows, 2 * group_width), "ctx")
    att_back, dq_back = pl.pallas_call(
        unpack_kernel,
        grid=(pairs,),
        in_specs=[pair_block],
        out_specs=[own_block, own_block],
        out_shape=[shape(queries.shape, bf16), shape(queries.shape, bf16)],
        name="unpack",
    )(both_back)

    grad_tokens = pl.pallas_call(
        token_kernel,
        grid_spec=pltpu.PrefetchScalarGridSpec(
            num_scalar_prefetch=1,
            grid=(n_ctx,),
            in_specs=[
                pl.BlockSpec((1, rows, pair_width), lambda j, p, c=c: (p[c], p[n_ctx], 0))
                for c in range(pairs)
            ]
            + [
                pl.BlockSpec((part, kv_width), lambda j, p: (j, 0)),
                pl.BlockSpec((part, kv_width), lambda j, p: (j, 0)),
                whole_block((all_rows, width)),
                pl.BlockSpec((all_rows, part), lambda j, p: (0, j)),
                pl.BlockSpec((1, part), lambda j, p: (0, j)),
                whole_block((all_rows, 1)),
            ],
            out_specs=whole_block((all_rows, width)),
            scratch_shapes=[
                pltpu.VMEM((all_rows, kv_width), bf16),
                pltpu.VMEM((all_rows, kv_width), bf16),
                pltpu.VMEM((n_ctx, all_rows, part), f32),
                pltpu.VMEM((all_rows, 1), f32),
            ],
        ),
        out_shape=shape((all_rows, width), bf16),
        name="tokens",
    )(
        source,
        *([pre_all] * pairs),
        key_weight,
        value_weight,
        flat,
        flat,
        gain_row,
        rms,
    )

    own = part // n_dp
    grad_key, grad_value, gain_sum = pl.pallas_call(
        last_kernel,
        grid_spec=pltpu.PrefetchScalarGridSpec(
            num_scalar_prefetch=1,
            grid=(1,),
            in_specs=[
                whole_block((n_dp, own, 2 * kv_width)),
                pl.BlockSpec((own, kv_width), lambda j, p: (p[0], 0)),
                pl.BlockSpec((own, kv_width), lambda j, p: (p[0], 0)),
            ],
            out_specs=[
                whole_block((own, kv_width)),
                whole_block((own, kv_width)),
                whole_block((own, 1)),
            ],
        ),
        out_shape=[shape((own, kv_width), f32), shape((own, kv_width), f32), shape((own, 1), f32)],
        name="last",
    )(slot, weight_in, key_weight, value_weight)
    own_gain = lax.dynamic_slice_in_dim(norm_gain, slot[0] * own, own, 0)
    grad_gain = gain_sum[:, 0] / own_gain
    return (
        att_back,
        dq_back,
        grad_tokens.reshape(seqs, rows, width),
        grad_key,
        grad_value,
        grad_gain,
    )


def body(tokens, queries, d_attended, span_order, norm_gain, key_weight, value_weight):
    pairs = tokens.shape[0] * (key_weight.shape[1] // HEAD_DIM)
    chosen = body_heads if pairs == lax.axis_size("ctx") else body_rows
    return chosen(tokens, queries, d_attended, span_order, norm_gain, key_weight, value_weight)


def solution(mesh):
    placed = (P("dp", "ctx", None), P("dp", "ctx", None), P("dp", "ctx", None), P(), P(), P(), P())
    return jax.shard_map(
        body,
        mesh=mesh,
        in_specs=placed,
        out_specs=(
            P("dp", "ctx", None),
            P("dp", "ctx", None),
            P("dp", "ctx", None),
            P(("ctx", "dp"), None),
            P(("ctx", "dp"), None),
            P(("ctx", "dp")),
        ),
        check_vma=False,
    )
```

```python
import jax
import jax.numpy as jnp
from jax import lax
from jax.experimental import pallas as pl
from jax.experimental.pallas import tpu as pltpu
from jax.sharding import PartitionSpec as P


KV_HEADS = 4
HEAD_DIM = 128


ROPE_BASE = 500000.0
EPSILON = 1e-05


def positions(span_order, span_len):
    offsets = jnp.arange(span_len, dtype=jnp.int32)
    return (span_order[:, None] * span_len + offsets[None, :]).reshape(-1)


def rotation(token_pos, head_size):
    half_dim = head_size // 2
    frequency = ROPE_BASE ** (-2.0 * jnp.arange(half_dim, dtype=jnp.float32) / head_size)
    angles = token_pos.astype(jnp.float32)[:, None] * frequency[None, :]
    angles = jnp.concatenate([angles, angles], axis=1)
    return (jnp.cos(angles), jnp.sin(angles))


def rotate_half(values):
    half_dim = values.shape[-1] // 2
    return jnp.concatenate([-values[..., half_dim:], values[..., :half_dim]], axis=-1)


def rotate_back(values):
    half_dim = values.shape[-1] // 2
    return jnp.concatenate([values[..., half_dim:], -values[..., :half_dim]], axis=-1)


def normalize(tokens, norm_gain):
    widened = tokens.astype(jnp.float32)
    rms_scale = lax.rsqrt(jnp.mean(widened * widened, axis=-1, keepdims=True) + EPSILON)
    return ((widened * rms_scale * norm_gain).astype(jnp.bfloat16), rms_scale)


def project_keys(normed, key_weight, value_weight, cosine, sine_table, kv_heads, head_size):
    row_count = normed.shape[0]
    key_pre = jnp.dot(normed, key_weight, preferred_element_type=jnp.float32).reshape(
        row_count, kv_heads, head_size
    )
    rotated = key_pre * cosine[:, None, :] + rotate_half(key_pre) * sine_table[:, None, :]
    value_rows = jnp.dot(normed, value_weight, preferred_element_type=jnp.float32)
    return (
        rotated.reshape(row_count, kv_heads * head_size).astype(jnp.bfloat16),
        value_rows.astype(jnp.bfloat16),
    )


def attend_group(query_group, grad_group, key_group, value_group, causal_mask, score_scale):
    scores = (
        jnp.einsum("tgd,sd->gts", query_group, key_group, preferred_element_type=jnp.float32)
        * score_scale
    )
    scores = jnp.where(causal_mask[None], scores, -1e30)
    row_max = jnp.max(scores, axis=-1, keepdims=True)
    exponent = jnp.exp(scores - row_max)
    probability = exponent / jnp.sum(exponent, axis=-1, keepdims=True)
    probability_b = probability.astype(jnp.bfloat16)
    attended = jnp.einsum(
        "gts,sd->tgd", probability_b, value_group, preferred_element_type=jnp.float32
    ).astype(jnp.bfloat16)
    dprob = jnp.einsum("tgd,sd->gts", grad_group, value_group, preferred_element_type=jnp.float32)
    delta = jnp.sum(grad_group.astype(jnp.float32) * attended.astype(jnp.float32), axis=-1)
    dscores = (probability * (dprob - jnp.transpose(delta)[:, :, None])).astype(jnp.bfloat16)
    dquery = (
        jnp.einsum("gts,sd->tgd", dscores, key_group, preferred_element_type=jnp.float32)
        * score_scale
    ).astype(jnp.bfloat16)
    key_term = (
        jnp.einsum("gts,tgd->sd", dscores, query_group, preferred_element_type=jnp.float32)
        * score_scale
    )
    value_term = jnp.einsum(
        "gts,tgd->sd", probability_b, grad_group, preferred_element_type=jnp.float32
    )
    return (attended, dquery, key_term, value_term)


def attend_device(queries, grads, all_keys, all_values, query_pos, key_pos, kv_heads, head_size):
    row_count = queries.shape[0]
    group_size = queries.shape[1] // (kv_heads * head_size)
    group_width = group_size * head_size
    causal_mask = key_pos[None, :] <= query_pos[:, None]
    score_scale = head_size ** (-0.5)
    outputs = []
    for head_group in range(kv_heads):
        query_group = queries[:, head_group * group_width : (head_group + 1) * group_width].reshape(
            row_count, group_size, head_size
        )
        grad_group = grads[:, head_group * group_width : (head_group + 1) * group_width].reshape(
            row_count, group_size, head_size
        )
        key_group = all_keys[:, head_group * head_size : (head_group + 1) * head_size]
        value_group = all_values[:, head_group * head_size : (head_group + 1) * head_size]
        outputs.append(
            attend_group(query_group, grad_group, key_group, value_group, causal_mask, score_scale)
        )
    attended = jnp.concatenate(
        [item[0].reshape(row_count, group_width) for item in outputs], axis=1
    )
    dquery = jnp.concatenate([item[1].reshape(row_count, group_width) for item in outputs], axis=1)
    key_terms = jnp.concatenate([item[2] for item in outputs], axis=1)
    value_terms = jnp.concatenate([item[3] for item in outputs], axis=1)
    return (attended, dquery, key_terms, value_terms)


def finish_backward(
    tokens,
    normed,
    rms_scale,
    key_grad,
    value_grad,
    cosine,
    sine_table,
    norm_gain,
    key_weight,
    value_weight,
    kv_heads,
    head_size,
):
    row_count = tokens.shape[0]
    shaped = key_grad.reshape(row_count, kv_heads, head_size)
    key_pre_grad = (
        (shaped * cosine[:, None, :] + rotate_back(shaped * sine_table[:, None, :]))
        .reshape(row_count, kv_heads * head_size)
        .astype(jnp.bfloat16)
    )
    value_pre_grad = value_grad.astype(jnp.bfloat16)
    weight_key = jnp.dot(normed.T, key_pre_grad, preferred_element_type=jnp.float32)
    weight_value = jnp.dot(normed.T, value_pre_grad, preferred_element_type=jnp.float32)
    normed_grad = jnp.dot(key_pre_grad, key_weight.T, preferred_element_type=jnp.float32) + jnp.dot(
        value_pre_grad, value_weight.T, preferred_element_type=jnp.float32
    )
    widened = tokens.astype(jnp.float32)
    gain_part = jnp.sum(normed_grad * widened * rms_scale, axis=0)
    inner_mean = jnp.mean(normed_grad * norm_gain * widened, axis=-1, keepdims=True)
    grad_rows = (
        rms_scale * norm_gain * normed_grad - widened * rms_scale**3 * inner_mean
    ).astype(jnp.bfloat16)
    return (grad_rows, weight_key, weight_value, gain_part)


def body_rows(tokens, queries, d_attended, span_order, norm_gain, key_weight, value_weight):
    local_seqs = tokens.shape[0]
    row_count = tokens.shape[1]
    model_width = tokens.shape[2]
    kv_width = key_weight.shape[1]
    shard_index = lax.axis_index("ctx")
    token_pos = positions(span_order, row_count // 2)
    query_pos = lax.dynamic_slice_in_dim(token_pos, shard_index * row_count, row_count, 0)
    cosine, sine_table = rotation(query_pos, HEAD_DIM)
    cosine_all = jnp.tile(cosine, (local_seqs, 1))
    sine_all = jnp.tile(sine_table, (local_seqs, 1))
    flat_tokens = tokens.reshape(local_seqs * row_count, model_width)
    normed, rms_scale = normalize(flat_tokens, norm_gain)
    rotated_keys, value_rows = project_keys(
        normed, key_weight, value_weight, cosine_all, sine_all, KV_HEADS, HEAD_DIM
    )
    rotated_keys = rotated_keys.reshape(local_seqs, row_count, kv_width)
    value_rows = value_rows.reshape(local_seqs, row_count, kv_width)
    all_keys, all_values = (
        lax.all_gather(rotated_keys, "ctx", axis=1, tiled=True),
        lax.all_gather(value_rows, "ctx", axis=1, tiled=True),
    )
    attended_list, dquery_list, key_list, value_list = ([], [], [], [])
    for sequence in range(local_seqs):
        attended, dquery, key_terms, value_terms = attend_device(
            queries[sequence],
            d_attended[sequence],
            all_keys[sequence],
            all_values[sequence],
            query_pos,
            token_pos,
            KV_HEADS,
            HEAD_DIM,
        )
        attended_list.append(attended)
        dquery_list.append(dquery)
        key_list.append(key_terms)
        value_list.append(value_terms)
    key_stack = jnp.stack(key_list)
    value_stack = jnp.stack(value_list)
    key_grad, value_grad = (
        lax.psum_scatter(
            key_stack.astype(jnp.bfloat16), "ctx", scatter_dimension=1, tiled=True
        ).astype(jnp.float32),
        lax.psum_scatter(
            value_stack.astype(jnp.bfloat16), "ctx", scatter_dimension=1, tiled=True
        ).astype(jnp.float32),
    )
    key_grad = key_grad.reshape(local_seqs * row_count, kv_width)
    value_grad = value_grad.reshape(local_seqs * row_count, kv_width)
    grad_rows, weight_key, weight_value, gain_part = finish_backward(
        flat_tokens,
        normed,
        rms_scale,
        key_grad,
        value_grad,
        cosine_all,
        sine_all,
        norm_gain,
        key_weight,
        value_weight,
        KV_HEADS,
        HEAD_DIM,
    )
    weight_key, weight_value, gain_part = (
        lax.psum_scatter(
            weight_key.astype(jnp.bfloat16), "ctx", scatter_dimension=0, tiled=True
        ).astype(jnp.float32),
        lax.psum_scatter(
            weight_value.astype(jnp.bfloat16), "ctx", scatter_dimension=0, tiled=True
        ).astype(jnp.float32),
        lax.psum_scatter(
            gain_part.astype(jnp.bfloat16), "ctx", scatter_dimension=0, tiled=True
        ).astype(jnp.float32),
    )
    weight_key, weight_value, gain_part = (
        lax.psum_scatter(
            weight_key.astype(jnp.bfloat16), "dp", scatter_dimension=0, tiled=True
        ).astype(jnp.float32),
        lax.psum_scatter(
            weight_value.astype(jnp.bfloat16), "dp", scatter_dimension=0, tiled=True
        ).astype(jnp.float32),
        lax.psum_scatter(
            gain_part.astype(jnp.bfloat16), "dp", scatter_dimension=0, tiled=True
        ).astype(jnp.float32),
    )
    return (
        jnp.stack(attended_list),
        jnp.stack(dquery_list),
        grad_rows.reshape(local_seqs, row_count, model_width),
        weight_key,
        weight_value,
        gain_part,
    )


NT = (((1,), (1,)), ((), ()))


def dot32(left, right):
    return jnp.dot(left, right, preferred_element_type=jnp.float32)


def project_kernel(
    place, tok_all, tok_part, gain, wk, wv, cosine, sine, normed_out, rms_out, kv_out, acc_k, acc_v, rms_s
):
    step = pl.program_id(0)
    pairs, seq_rows, pair_width = kv_out.shape
    head = pair_width // 2

    @pl.when(step == 0)
    def _():
        wide = tok_all[...].astype(jnp.float32)
        rms_s[...] = lax.rsqrt(jnp.mean(wide * wide, axis=-1, keepdims=True) + EPSILON)
        rms_out[...] = rms_s[...]
        acc_k[...] = jnp.zeros_like(acc_k)
        acc_v[...] = jnp.zeros_like(acc_v)

    normed = (tok_part[...].astype(jnp.float32) * rms_s[...] * gain[...]).astype(jnp.bfloat16)
    normed_out[0] = normed
    acc_k[...] += dot32(normed, wk[...])
    acc_v[...] += dot32(normed, wv[...])

    @pl.when(step == pl.num_programs(0) - 1)
    def _():
        kv_heads = acc_k.shape[1] // head
        for group in range(kv_heads):
            columns = slice(group * head, (group + 1) * head)
            key_pre = acc_k[:, columns]
            rotated = key_pre * cosine[...] - pltpu.roll(key_pre, head // 2, 1) * sine[...]
            rotated = rotated.astype(jnp.bfloat16)
            value = acc_v[:, columns].astype(jnp.bfloat16)
            for seq in range(pairs // kv_heads):
                rows = slice(seq * seq_rows, (seq + 1) * seq_rows)
                kv_out[seq * kv_heads + group, :, :head] = rotated[rows]
                kv_out[seq * kv_heads + group, :, head:] = value[rows]


def attend_kernel(
    query, grad, kv, cosine, sine, key_pos, query_pos, both_out, pre_out, acc_k, acc_v
):
    step = pl.program_id(0)
    head = query.shape[1]
    scale = head ** (-0.5)

    @pl.when(step == 0)
    def _():
        acc_k[...] = jnp.zeros_like(acc_k)
        acc_v[...] = jnp.zeros_like(acc_v)

    q = query[...]
    g = grad[...]
    k = kv[:, :head]
    v = kv[:, head:]
    grad_t = g.T
    scores = lax.dot_general(k, q, NT, preferred_element_type=jnp.float32) * scale
    scores = jnp.where(key_pos[...] <= query_pos[...], scores, -1e30)
    exponent = jnp.exp(scores - jnp.max(scores, axis=0, keepdims=True))
    prob = exponent * (1.0 / jnp.sum(exponent, axis=0, keepdims=True))
    prob_b = prob.astype(jnp.bfloat16)
    att_t = dot32(v.T, prob_b)
    both_out[:, :head] = att_t.T.astype(jnp.bfloat16)
    att_r = att_t.astype(jnp.bfloat16).astype(jnp.float32)
    delta = jnp.sum(att_r * grad_t.astype(jnp.float32), axis=0, keepdims=True)
    dprob = dot32(v, grad_t)
    dscores = (prob * (dprob - delta)).astype(jnp.bfloat16)
    both_out[:, head:] = (dot32(k.T, dscores) * scale).T.astype(jnp.bfloat16)
    acc_k[...] += dot32(dscores, q)
    acc_v[...] += dot32(prob_b, g)

    @pl.when(step == pl.num_programs(0) - 1)
    def _():
        key_grad = acc_k[...] * scale
        back = key_grad * cosine[...] + pltpu.roll(key_grad, head // 2, 1) * sine[...]
        pre_out[:, :head] = back.astype(jnp.bfloat16)
        pre_out[:, head:] = acc_v[...].astype(jnp.bfloat16)


def pack_kernel(query, grad, out):
    width = query.shape[2]
    out[0, :, :width] = query[0]
    out[0, :, width:] = grad[0]


def unpack_kernel(both, att, dq):
    for h in range(att.shape[2] // HEAD_DIM):
        columns = slice(h * HEAD_DIM, (h + 1) * HEAD_DIM)
        first = 2 * h * HEAD_DIM
        att[0, :, columns] = both[0, :, first : first + HEAD_DIM]
        dq[0, :, columns] = both[0, :, first + HEAD_DIM : first + 2 * HEAD_DIM]


def weight_kernel(place, *refs):
    *inputs, out, stacked, turned = refs
    seqs, seq, _ = stacked.shape
    pre, normed = inputs[:seqs], inputs[seqs:]
    rows = seq // len(normed)

    @pl.when(pl.program_id(0) == 0)
    def _():
        for s in range(seqs):
            for c, block in enumerate(normed):
                stacked[s, c * rows : (c + 1) * rows] = block[0, s]
            turned[s] = stacked[s].T

    total = dot32(turned[0], pre[0][0])
    for s in range(1, seqs):
        total += dot32(turned[s], pre[s][0])
    out[...] = total.astype(jnp.bfloat16).reshape(out.shape)


def token_kernel(place, *refs):
    *pre, wk, wv, tok_all, tok_part, gain_part, rms, out, pk, pv, ng, inner = refs
    step = pl.program_id(0)
    rows, pair_width = pre[0].shape[1:]
    head = pair_width // 2
    kv_heads = pk.shape[1] // head
    seqs = pk.shape[0] // rows

    @pl.when(step == 0)
    def _():
        for s in range(seqs):
            for h in range(kv_heads):
                pk[s * rows : (s + 1) * rows, h * head : (h + 1) * head] = pre[s * kv_heads + h][0, :, :head]
                pv[s * rows : (s + 1) * rows, h * head : (h + 1) * head] = pre[s * kv_heads + h][0, :, head:]
        inner[...] = jnp.zeros_like(inner)

    grad = lax.dot_general(pk[...], wk[...], NT, preferred_element_type=jnp.float32)
    grad += lax.dot_general(pv[...], wv[...], NT, preferred_element_type=jnp.float32)
    grad = grad * gain_part[...]
    ng[step] = grad
    inner[...] += jnp.sum(grad * tok_part[...].astype(jnp.float32), axis=-1, keepdims=True)

    @pl.when(step == pl.num_programs(0) - 1)
    def _():
        scale = rms[...]
        factor = scale * scale * scale * (inner[...] / tok_all.shape[1])
        width = ng.shape[2]
        for j in range(ng.shape[0]):
            part = slice(j * width, (j + 1) * width)
            wide = tok_all[:, part].astype(jnp.float32)
            out[:, part] = (scale * ng[j] - wide * factor).astype(jnp.bfloat16)


def last_kernel(place, parts, wk, wv, gk, gv, gain):
    total = parts[0].astype(jnp.float32)
    for i in range(1, parts.shape[0]):
        total += parts[i].astype(jnp.float32)
    kv_width = gk.shape[1]
    head = HEAD_DIM
    gain_sum = jnp.zeros((gk.shape[0], head), jnp.float32)
    for h in range(kv_width // head):
        columns = slice(h * head, (h + 1) * head)
        key_part = total[:, 2 * h * head : (2 * h + 1) * head]
        value_part = total[:, (2 * h + 1) * head : (2 * h + 2) * head]
        gk[:, columns] = key_part
        gv[:, columns] = value_part
        gain_sum += key_part * wk[:, columns].astype(jnp.float32)
        gain_sum += value_part * wv[:, columns].astype(jnp.float32)
    gain[...] = jnp.sum(gain_sum, axis=-1, keepdims=True)


def shape(dims, kind):
    return jax.ShapeDtypeStruct(dims, kind)


def whole_block(dims):
    return pl.BlockSpec(dims, lambda *_: (0,) * len(dims))


def exchange(values, axis):
    return lax.all_to_all(values, axis, split_axis=0, concat_axis=0, tiled=True)


def shifted(blocks):
    count = len(blocks)
    moved = [blocks[0]]
    for d in range(1, count):
        moved.append(lax.ppermute(blocks[d], "ctx", [(i, (i + d) % count) for i in range(count)]))
    return moved


def body_heads(tokens, queries, d_attended, span_order, norm_gain, key_weight, value_weight):
    bf16, f32 = jnp.bfloat16, jnp.float32
    seqs, rows, width = tokens.shape
    kv_width = key_weight.shape[1]
    kv_heads = kv_width // HEAD_DIM
    n_ctx = lax.axis_size("ctx")
    n_dp = lax.axis_size("dp")
    pairs = seqs * kv_heads
    seq = rows * n_ctx
    group_width = queries.shape[2] // kv_heads
    heads = group_width // HEAD_DIM
    part = width // n_ctx
    all_rows = seqs * rows
    pair_width = 2 * HEAD_DIM
    place = lax.axis_index("ctx").astype(jnp.int32)
    slot = (place * n_dp + lax.axis_index("dp").astype(jnp.int32)).reshape(1)

    own_block = pl.BlockSpec((1, rows, group_width), lambda i: (i // kv_heads, 0, i % kv_heads))
    pair_block = pl.BlockSpec((1, rows, 2 * group_width), lambda i: (i, 0, 0))
    both = pl.pallas_call(
        pack_kernel,
        grid=(pairs,),
        in_specs=[own_block, own_block],
        out_specs=pair_block,
        out_shape=shape((pairs, rows, 2 * group_width), bf16),
        name="pack",
    )(queries, d_attended)

    token_pos = positions(span_order, rows // 2)
    cosine, sine = rotation(token_pos, HEAD_DIM)
    sign = jnp.where(jnp.arange(HEAD_DIM) < HEAD_DIM // 2, 1.0, -1.0).astype(f32)
    sine = sine * sign[None, :]
    own_cos = jnp.tile(lax.dynamic_slice_in_dim(cosine, place * rows, rows, 0), (seqs, 1))
    own_sin = jnp.tile(lax.dynamic_slice_in_dim(sine, place * rows, rows, 0), (seqs, 1))
    flat = tokens.reshape(all_rows, width)
    both, flat = lax.optimization_barrier((both, flat))
    both_in = exchange(both, "ctx").reshape(seq, 2 * group_width)
    gain_row = norm_gain[None, :]

    normed, rms, kv = pl.pallas_call(
        project_kernel,
        grid_spec=pltpu.PrefetchScalarGridSpec(
            num_scalar_prefetch=1,
            grid=(n_ctx,),
            in_specs=[
                whole_block((all_rows, width)),
                pl.BlockSpec((all_rows, part), lambda j, p: (0, j)),
                pl.BlockSpec((1, part), lambda j, p: (0, j)),
                pl.BlockSpec((part, kv_width), lambda j, p: (j, 0)),
                pl.BlockSpec((part, kv_width), lambda j, p: (j, 0)),
                whole_block((all_rows, HEAD_DIM)),
                whole_block((all_rows, HEAD_DIM)),
            ],
            out_specs=[
                pl.BlockSpec(
                    (1, all_rows, part), lambda j, p: (lax.rem(j - p[0] + n_ctx, n_ctx), 0, 0)
                ),
                whole_block((all_rows, 1)),
                whole_block((pairs, rows, pair_width)),
            ],
            scratch_shapes=[
                pltpu.VMEM((all_rows, kv_width), f32),
                pltpu.VMEM((all_rows, kv_width), f32),
                pltpu.VMEM((all_rows, 1), f32),
            ],
        ),
        out_shape=[
            shape((n_ctx, all_rows, part), bf16),
            shape((all_rows, 1), f32),
            shape((pairs, rows, pair_width), bf16),
        ],
        cost_estimate=pl.CostEstimate(flops=4 * all_rows * width * kv_width, bytes_accessed=0, transcendentals=0),
        name="project",
    )(place.reshape(1), flat, flat, gain_row, key_weight, value_weight, own_cos, own_sin)

    kv, normed, both_in = lax.optimization_barrier((kv, normed, both_in))
    kv_in = exchange(kv, "ctx").reshape(seq, pair_width)
    normed_in = shifted([normed[d] for d in range(n_ctx)])
    normed_in = [block.reshape(seqs, rows, part) for block in normed_in]
    normed_in = jnp.stack(normed_in)
    source = lax.rem(place - jnp.arange(n_ctx, dtype=jnp.int32) + n_ctx, n_ctx)
    source = jnp.concatenate([source, place.reshape(1)])

    both_out, pre = pl.pallas_call(
        attend_kernel,
        grid=(heads,),
        in_specs=[
            pl.BlockSpec((seq, HEAD_DIM), lambda h: (0, h)),
            pl.BlockSpec((seq, HEAD_DIM), lambda h: (0, heads + h)),
            whole_block((seq, pair_width)),
            whole_block((seq, HEAD_DIM)),
            whole_block((seq, HEAD_DIM)),
            whole_block((seq, 1)),
            whole_block((1, seq)),
        ],
        out_specs=[
            pl.BlockSpec((seq, pair_width), lambda h: (0, h)),
            whole_block((seq, pair_width)),
        ],
        out_shape=[
            shape((seq, 2 * group_width), bf16),
            shape((seq, pair_width), bf16),
        ],
        scratch_shapes=[pltpu.VMEM((seq, HEAD_DIM), f32), pltpu.VMEM((seq, HEAD_DIM), f32)],
        cost_estimate=pl.CostEstimate(flops=16 * heads * seq * seq * HEAD_DIM, bytes_accessed=0, transcendentals=0),
        name="attend",
    )(both_in, both_in, kv_in, cosine, sine, token_pos[:, None], token_pos[None, :])

    pre_all = jnp.stack(shifted([pre] * n_ctx))

    weight_parts = pl.pallas_call(
        weight_kernel,
        grid_spec=pltpu.PrefetchScalarGridSpec(
            num_scalar_prefetch=1,
            grid=(kv_heads,),
            in_specs=[
                pl.BlockSpec((1, seq, pair_width), lambda h, p, s=s: (p[s * kv_heads + h], 0, 0))
                for s in range(seqs)
            ]
            + [
                pl.BlockSpec((1, seqs, rows, part), lambda h, p, c=c: (p[c], 0, 0, 0))
                for c in range(n_ctx)
            ],
            out_specs=pl.BlockSpec((n_dp, part // n_dp, pair_width), lambda h, p: (0, 0, h)),
            scratch_shapes=[
                pltpu.VMEM((seqs, seq, part), bf16),
                pltpu.VMEM((seqs, part, seq), bf16),
            ],
        ),
        out_shape=shape((n_dp, part // n_dp, 2 * kv_width), bf16),
        cost_estimate=pl.CostEstimate(flops=4 * seqs * seq * part * kv_width, bytes_accessed=0, transcendentals=0),
        name="weights",
    )(source, *([pre_all] * seqs), *([normed_in] * n_ctx))
    weight_in = exchange(weight_parts, "dp")

    both_back = exchange(both_out.reshape(n_ctx, rows, 2 * group_width), "ctx")
    att_back, dq_back = pl.pallas_call(
        unpack_kernel,
        grid=(pairs,),
        in_specs=[pair_block],
        out_specs=[own_block, own_block],
        out_shape=[shape(queries.shape, bf16), shape(queries.shape, bf16)],
        name="unpack",
    )(both_back)

    grad_tokens = pl.pallas_call(
        token_kernel,
        grid_spec=pltpu.PrefetchScalarGridSpec(
            num_scalar_prefetch=1,
            grid=(n_ctx,),
            in_specs=[
                pl.BlockSpec((1, rows, pair_width), lambda j, p, c=c: (p[c], p[n_ctx], 0))
                for c in range(pairs)
            ]
            + [
                pl.BlockSpec((part, kv_width), lambda j, p: (j, 0)),
                pl.BlockSpec((part, kv_width), lambda j, p: (j, 0)),
                whole_block((all_rows, width)),
                pl.BlockSpec((all_rows, part), lambda j, p: (0, j)),
                pl.BlockSpec((1, part), lambda j, p: (0, j)),
                whole_block((all_rows, 1)),
            ],
            out_specs=whole_block((all_rows, width)),
            scratch_shapes=[
                pltpu.VMEM((all_rows, kv_width), bf16),
                pltpu.VMEM((all_rows, kv_width), bf16),
                pltpu.VMEM((n_ctx, all_rows, part), f32),
                pltpu.VMEM((all_rows, 1), f32),
            ],
        ),
        out_shape=shape((all_rows, width), bf16),
        cost_estimate=pl.CostEstimate(flops=4 * all_rows * width * kv_width, bytes_accessed=0, transcendentals=0),
        name="tokens",
    )(
        source,
        *([pre_all] * pairs),
        key_weight,
        value_weight,
        flat,
        flat,
        gain_row,
        rms,
    )

    own = part // n_dp
    grad_key, grad_value, gain_sum = pl.pallas_call(
        last_kernel,
        grid_spec=pltpu.PrefetchScalarGridSpec(
            num_scalar_prefetch=1,
            grid=(1,),
            in_specs=[
                whole_block((n_dp, own, 2 * kv_width)),
                pl.BlockSpec((own, kv_width), lambda j, p: (p[0], 0)),
                pl.BlockSpec((own, kv_width), lambda j, p: (p[0], 0)),
            ],
            out_specs=[
                whole_block((own, kv_width)),
                whole_block((own, kv_width)),
                whole_block((own, 1)),
            ],
        ),
        out_shape=[shape((own, kv_width), f32), shape((own, kv_width), f32), shape((own, 1), f32)],
        name="last",
    )(slot, weight_in, key_weight, value_weight)
    own_gain = lax.dynamic_slice_in_dim(norm_gain, slot[0] * own, own, 0)
    grad_gain = gain_sum[:, 0] / own_gain
    return (
        att_back,
        dq_back,
        grad_tokens.reshape(seqs, rows, width),
        grad_key,
        grad_value,
        grad_gain,
    )


def body(tokens, queries, d_attended, span_order, norm_gain, key_weight, value_weight):
    pairs = tokens.shape[0] * (key_weight.shape[1] // HEAD_DIM)
    chosen = body_heads if pairs == lax.axis_size("ctx") else body_rows
    return chosen(tokens, queries, d_attended, span_order, norm_gain, key_weight, value_weight)


def solution(mesh):
    placed = (P("dp", "ctx", None), P("dp", "ctx", None), P("dp", "ctx", None), P(), P(), P(), P())
    return jax.shard_map(
        body,
        mesh=mesh,
        in_specs=placed,
        out_specs=(
            P("dp", "ctx", None),
            P("dp", "ctx", None),
            P("dp", "ctx", None),
            P(("ctx", "dp"), None),
            P(("ctx", "dp"), None),
            P(("ctx", "dp")),
        ),
        check_vma=False,
    )
```
